32 devices in a mesh: sn: 8 (over y, x, core), blk: 4 (over z).
Axes of the slice: x: 2, y: 2, z: 4, core: 2. Of those that a mesh axis runs over, the one named last changes fastest.
Arguments:
- root_inverse: float32 [2048, 2048], P('sn'), as said below
- structure: int32 [8, 4], replicated, may hold values from 0 to 7, as said below
- panel_one: float32 [8, 1024, 256], P('sn', 'blk'), may hold values from -0.375 to 0.375
- inverse_one: float32 [8, 256, 256], P('sn'), as said below
- parent_two: float32 [8, 256, 256], P('sn'), may hold values from -0.375 to 0.375
- panel_two: float32 [8, 1024, 256], P('sn', 'blk'), may hold values from -0.375 to 0.375
- inverse_two: float32 [8, 256, 256], P('sn'), as said below
Outputs:
- sigma_diag_one: float32 [8, 256, 256], P('sn')
- sigma_off_one: float32 [8, 1024, 256], P('sn', 'blk')
- sigma_diag_two: float32 [8, 256, 256], P('sn')
- sigma_par_two: float32 [8, 256, 256], P('sn')
- sigma_root_two: float32 [8, 1024, 256], P('sn', 'blk')
The draws below stay inside these ranges and needn't reach their ends.
Inputs may be any that keep to these rules, and one draw needn't show every extreme that they name: `structure`: each row holds 4 distinct block indices. `inverse_one`: lower triangular; diagonal between 0.5 and 1.5. `inverse_two`: lower triangular; diagonal between 0.5 and 1.5. `root_inverse`: Symmetric.
All inputs are finite; a program needn't handle non-finite values.
Results may differ from the reference program's by a relative error of at most 0.00011.
Values sent between devices are 32-bit elements; how exact they have to be, the bound alone decides.
No kernel may reach another device: no remote copies, remote signals or barrier semaphores. Data moves between devices by JAX's collectives and lax.ppermute only.
A program may use at most 128 MiB of HBM per device.

```python
import math
import jax
import jax.numpy as jnp
from jax import lax

B = 256
K = 4
RB = 8
SUPER = 8


def draw_root_inverse(key, part):
    total = RB * B
    first, second, third = jax.random.split(key, 3)
    base = jax.random.normal(first, (total, total), jnp.float32)
    scale = jnp.exp(jax.random.uniform(second, (total,), jnp.float32, 0.0, math.log(3.0)))
    coupling = (base + base.T) * (1.4142 / math.sqrt(total))
    diagonal = jax.random.uniform(third, (total,), jnp.float32, 1.0, 4.0)
    rows = jnp.arange(total)[:, None]
    cols = jnp.arange(total)[None, :]
    middle = jnp.where(rows == cols, diagonal[:, None], coupling)
    return scale[:, None] * middle * scale[None, :]


def draw_structure(key, part):
    first, second = jax.random.split(key, 2)
    order = jax.random.permutation(first, RB)
    starts = jax.random.randint(second, (SUPER,), 0, RB)
    rows = jnp.arange(SUPER)
    starts = jnp.where(rows < RB // K, rows * K, starts)
    places = (starts[:, None] + jnp.arange(K)[None, :]) % RB
    return order[places].astype(jnp.int32)


def lower_inverse(key):
    first, second = jax.random.split(key, 2)
    body_part = jax.random.normal(first, (SUPER, B, B), jnp.float32) * (0.5 / math.sqrt(B))
    diagonal = jax.random.uniform(second, (SUPER, B), jnp.float32, 0.5, 1.5)
    rows = jnp.arange(B)[:, None]
    cols = jnp.arange(B)[None, :]
    strict = jnp.where(rows > cols, body_part, 0.0)
    return jnp.where(rows == cols, diagonal[:, :, None], strict)


def draw_inverse_one(key, part):
    return lower_inverse(jax.random.fold_in(key, 11))


def draw_inverse_two(key, part):
    return lower_inverse(jax.random.fold_in(key, 23))


def steps_of(rng, dims, cuts, smallest, largest):
    gain, own = 1.0, jax.random.fold_in(rng, 6)
    for position, parts in cuts:
        draws = jnp.exp(jax.random.uniform(jax.random.fold_in(own, position), (parts,), jnp.float32, smallest / len(cuts), largest / len(cuts)))
        gain = gain * jnp.repeat(draws, dims[position] // parts).reshape([-1 if axis == position else 1 for axis in range(len(dims))])
    return gain


def bell_draw(own_key, dims, scale, limit, pieces=(), held_as=jnp.bfloat16):
    gain = steps_of(own_key, dims, pieces, -0.22, 0.18) if pieces else 1.0
    entries = jax.random.normal(own_key, dims, jnp.float32) * scale * gain
    return jnp.minimum(jnp.maximum(entries, -limit), limit).astype(held_as)


def setup_inputs(seed: int = 0) -> dict:
    streams_of = jax.random.split(jax.random.key(seed), 8)
    root_inverse = draw_root_inverse(jax.random.fold_in(streams_of[7], 71), 0)
    structure = draw_structure(jax.random.fold_in(streams_of[7], 71), 0)
    panel_one = bell_draw(streams_of[2], (SUPER, K * B, B), B ** -0.5, 0.375, ((0, 8), (1, 4)), jnp.float32)
    inverse_one = draw_inverse_one(jax.random.fold_in(streams_of[7], 71), 0)
    parent_two = bell_draw(streams_of[4], (SUPER, B, B), B ** -0.5, 0.375, ((0, 8),), jnp.float32)
    panel_two = bell_draw(streams_of[5], (SUPER, K * B, B), B ** -0.5, 0.375, ((0, 8), (1, 4)), jnp.float32)
    inverse_two = draw_inverse_two(jax.random.fold_in(streams_of[7], 71), 0)
    return dict(root_inverse=root_inverse, structure=structure, panel_one=panel_one, inverse_one=inverse_one, parent_two=parent_two, panel_two=panel_two, inverse_two=inverse_two)


def product(left, right):
    return jnp.dot(left, right, precision=lax.Precision.HIGHEST, preferred_element_type=jnp.float32)


def reference(root_inverse, structure, panel_one, inverse_one, parent_two, panel_two, inverse_two):
    blocks = root_inverse.reshape(RB, B, RB, B)

    def single(items):
        listed, lower_one, inv_one, upper_two, lower_two, inv_two = items
        picked = jnp.take(blocks, listed, axis=0)
        picked = jnp.take(picked, listed, axis=2).reshape(K * B, K * B)
        u_one = product(lower_one, inv_one)
        u_root = product(lower_two, inv_two)
        u_par = product(upper_two, inv_two)
        w_all = product(picked, jnp.concatenate([u_one, u_root], axis=1))
        w_one = w_all[:, :B]
        w_two = w_all[:, B:]
        off_one = -w_one
        diag_one = product(inv_one.T, inv_one) + product(u_one.T, w_one)
        root_two = -(w_two + product(off_one, u_par))
        par_two = -(product(off_one.T, u_root) + product(diag_one, u_par))
        diag_two = product(inv_two.T, inv_two) - product(u_par.T, par_two) - product(u_root.T, root_two)
        return diag_one, off_one, diag_two, par_two, root_two

    outs = lax.map(single, (structure, panel_one, inverse_one, parent_two, panel_two, inverse_two))
    return (outs[0], outs[1], outs[2], outs[3], outs[4])
```

```python
import functools
import jax
import jax.numpy as jnp
from jax import lax
from jax.experimental import pallas as pl
from jax.experimental.pallas import tpu as pltpu
from jax.sharding import PartitionSpec as P


AXES = ("sn", "blk")
ANY = pl.BlockSpec(memory_space=pl.ANY)
VMEM = pl.BlockSpec(memory_space=pltpu.VMEM)
SMEM = pl.BlockSpec(memory_space=pltpu.SMEM)
ROWS = (((0,), (0,)), ((), ()))
INNER = (((1,), (0,)), ((), ()))


def split(x):
    high = x.astype(jnp.bfloat16)
    return high, (x - high.astype(jnp.float32)).astype(jnp.bfloat16)


def mul(left, right, dims=INNER):
    dot = functools.partial(lax.dot_general, dimension_numbers=dims, preferred_element_type=jnp.float32)
    return dot(left[0], right[0]) + (dot(left[0], right[1]) + dot(left[1], right[0]))


def flip(i, bits):
    for bit in (1, 2):
        if bits & bit:
            i = i + bit - 2 * bit * ((i // bit) % 2)
    return i


def place(groups):
    half = groups // 2
    owner, plane = lax.axis_index("sn"), lax.axis_index("blk")
    core = owner % 2
    home = plane // half
    return owner, plane, core, home, 2 * (plane % half) + core


def send_kernel(groups, width, structure, root, one, two, out, pack):
    half = groups // 2
    _, plane, _, home, _ = place(groups)
    rows = width // groups
    for target in range(structure.shape[0]):
        node = target - target % 2 + home
        piece = 2 * (plane % half) + target % 2
        for k in range(structure.shape[1]):
            block = structure[node, k]
            out[target, :, k * width : (k + 1) * width] = root[
                pl.ds(pl.multiple_of(piece * rows, rows), rows), pl.ds(pl.multiple_of(block * width, width), width)
            ]
    pack[:, :width] = one[0]
    pack[:, width:] = two[0]


def main_kernel(groups, structure, recv, own, lent, first, second, swapped, passed,
                y0, y1, y2, y3, g0, g1, g2, g3, square, panels, product, mixed, cross, corner, part, sems):
    count, width = structure.shape[1], panels.shape[0] // structure.shape[1]
    rows = width // groups
    owner, plane, core, home, piece = place(groups)
    node = owner - core + home
    near = core == home
    starts = []
    for k in range(count):
        copy = pltpu.make_async_copy(recv.at[structure[node, k]], square.at[pl.ds(k * rows, rows), :], sems.at[k])
        copy.start()
        starts.append(copy)
    mirror = groups - 1 - plane
    places = (plane, flip(plane, 1), mirror, flip(mirror, 1))
    slots = [panels.at[pl.ds(pl.multiple_of(p * width, width), width), :] for p in places]

    def take(sources):
        for i, source in enumerate(sources):
            pltpu.make_async_copy(source, slots[i], sems.at[count + i]).start()

    @pl.when(near)
    def _():
        take((own, swapped, first, passed))

    @pl.when(jnp.logical_not(near))
    def _():
        take((lent, first, swapped, second))

    for copy in starts:
        copy.wait()
    for i in range(groups):
        pltpu.make_async_copy(own, slots[i], sems.at[count + i]).wait()
    product[...] = mul(split(square[...]), split(panels[...]))
    for i, y in enumerate((y0, y1, y2, y3)):
        k = flip(piece, i)
        y[...] = product[pl.ds(pl.multiple_of(k * rows, rows), rows), :]
    for k in range(count):
        part[k * rows : (k + 1) * rows, :] = panels[pl.ds(pl.multiple_of(k * width + piece * rows, rows), rows), :]
    p_one, p_two = split(part[:, :width]), split(part[:, width:])
    w_one, w_two = split(product[:, :width]), split(product[:, width:])
    over_one = mul(p_one, w_one, ROWS)
    over_two = mul(p_two, w_two, ROWS)
    cross[...] = mul(p_one, w_two, ROWS)
    row = lax.broadcasted_iota(jnp.int32, (width, width), 0)
    col = lax.broadcasted_iota(jnp.int32, (width, width), 1)
    mixed[...] = jnp.where(row >= col, over_one, over_two)
    corner[...] = jnp.where(row == col, over_two, 0.0)
    for i, g in enumerate((g0, g1, g2, g3)):
        window = pl.ds(pl.multiple_of(flip(piece, i) * rows, rows), rows)
        g[:rows, :] = mixed[window, :]
        g[rows : 2 * rows, :] = cross[window, :]
        g[2 * rows :, :] = jnp.broadcast_to(jnp.sum(corner[window, :], axis=0, keepdims=True), (8, width))


def panel_kernel(groups, y0, y1, y2, y3, one, two, parent, off, root, u_par, rows_of):
    width = one.shape[-1]
    rows = width // groups
    plane = lax.axis_index("blk")
    for i, y in enumerate((y0, y1, y2, y3)):
        rows_of[pl.ds(pl.multiple_of(flip(plane, i) * rows, rows), rows), :] = y[...]
    inv_two = split(two[0])
    u = mul(split(parent[0]), inv_two)
    u_par[...] = u
    w_one = mul(split(rows_of[:, :width]), split(one[0]))
    off[0] = -w_one
    w_two = mul(split(rows_of[:, width:]), inv_two)
    root[0] = mul(split(w_one), split(u)) - w_two


def diag_kernel(groups, g0, g1, g2, g3, one, two, u_par, diag_one, diag_two, par_two, mixed, cross):
    width = one.shape[-1]
    rows = width // groups
    plane = lax.axis_index("blk")
    corner = jnp.zeros((1, width), jnp.float32)
    for i, g in enumerate((g0, g1, g2, g3)):
        window = pl.ds(pl.multiple_of(flip(plane, i) * rows, rows), rows)
        mixed[window, :] = g[:rows, :]
        cross[window, :] = g[rows : 2 * rows, :]
        corner = corner + g[2 * rows : 2 * rows + 1, :]
    row = lax.broadcasted_iota(jnp.int32, (width, width), 0)
    col = lax.broadcasted_iota(jnp.int32, (width, width), 1)
    eye = jnp.where(row == col, 1.0, 0.0)
    both = mixed[...]
    turned = both.T
    over_one = jnp.where(row >= col, both, turned) + eye
    over_two = jnp.where(row == col, corner + 1.0, jnp.where(row < col, both, turned))
    inv_one, inv_two, u = split(one[0]), split(two[0]), split(u_par[...])
    sigma = mul(inv_one, split(mul(split(over_one), inv_one)), ROWS)
    diag_one[0] = sigma
    middle = mul(inv_one, split(mul(split(cross[...]), inv_two)), ROWS)
    coupled = middle - mul(split(sigma), u)
    par_two[0] = coupled
    last = mul(inv_two, split(mul(split(over_two), inv_two)), ROWS)
    diag_two[0] = last - mul(split(middle), u, ROWS) - mul(u, split(coupled), ROWS)


def f32(*shape):
    return jax.ShapeDtypeStruct(shape, jnp.float32)


def cost(flops, size):
    return pl.CostEstimate(flops=flops, bytes_accessed=size, transcendentals=0)


def routes(nodes, groups):
    half = groups // 2

    def route(step):
        pairs = []
        for owner in range(nodes):
            core, column = owner % 2, owner - owner % 2
            for plane in range(groups):
                home = plane // half
                piece = 2 * (plane % half) + core
                target = step(core, plane, home, piece)
                if target is not None:
                    pairs.append((owner * groups + plane, (column + target[0]) * groups + target[1]))
        return pairs

    def near(core, home):
        return core == home

    table = {
        "first": route(lambda c, z, h, q: (1 - c, z ^ 1) if near(c, h) else (c, groups - 1 - z)),
        "second": route(lambda c, z, h, q: None if near(c, h) else (1 - c, (groups - 1 - z) ^ 1)),
        "lend": route(lambda c, z, h, q: (1 - c, z) if near(c, h) else None),
        "pass": route(lambda c, z, h, q: None if near(c, h) else (1 - c, z)),
        "swap": route(lambda c, z, h, q: (1 - c, z)),
        "reduce": [None]
        + [route(lambda c, z, h, q, i=i: (c ^ (i & 1), z ^ (i >> 1))) for i in range(1, groups)],
        "spread": [route(lambda c, z, h, q, i=i: (h, q ^ i)) for i in range(groups)],
    }
    return table


def per_device(root_inverse, structure, panel_one, inverse_one, parent_two, panel_two, inverse_two):
    width = inverse_one.shape[-1]
    nodes, groups = lax.axis_size("sn"), lax.axis_size("blk")
    count = structure.shape[1]
    rows = width // groups
    table = routes(nodes, groups)
    move = lambda x, pairs: lax.ppermute(x, AXES, pairs)

    outgoing, own = pl.pallas_call(
        functools.partial(send_kernel, groups, width),
        name="send",
        out_shape=(f32(nodes, rows, count * width), f32(width, 2 * width)),
        in_specs=[SMEM, VMEM, VMEM, VMEM],
        out_specs=(VMEM, VMEM),
        cost_estimate=cost(0, 2 * 4 * root_inverse.size),
    )(structure, root_inverse, panel_one, panel_two)
    recv = lax.all_to_all(outgoing, "sn", split_axis=0, concat_axis=0, tiled=True)
    lent = move(own, table["lend"])
    first = move(own, table["first"])
    second = move(own, table["second"])
    swapped = move(first, table["swap"])
    passed = move(second, table["pass"])

    ys_gs = pl.pallas_call(
        functools.partial(main_kernel, groups),
        name="main",
        out_shape=(f32(rows, 2 * width),) * groups + (f32(2 * rows + 8, width),) * groups,
        in_specs=[SMEM] + [ANY] * 7,
        out_specs=(VMEM,) * (2 * groups),
        scratch_shapes=[
            pltpu.VMEM((count * rows, count * width), jnp.float32),
            pltpu.VMEM((count * width, 2 * width), jnp.float32),
            pltpu.VMEM((count * rows, 2 * width), jnp.float32),
            pltpu.VMEM((width, width), jnp.float32),
            pltpu.VMEM((width, width), jnp.float32),
            pltpu.VMEM((width, width), jnp.float32),
            pltpu.VMEM((count * rows, 2 * width), jnp.float32),
            pltpu.SemaphoreType.DMA((count + groups,)),
        ],
        cost_estimate=cost(2 * 3 * width**3 * 11, 4 * 14 * width * width),
    )(structure, recv, own, lent, first, second, swapped, passed)
    ys, gs = ys_gs[:groups], ys_gs[groups:]
    total = gs[0]
    for i in range(1, groups):
        total = total + move(gs[i], table["reduce"][i])
    ys = [move(ys[i], table["spread"][i]) for i in range(groups)]
    totals = [move(total, table["spread"][i]) for i in range(groups)]
    off_one, root_two, u_par = pl.pallas_call(
        functools.partial(panel_kernel, groups),
        name="panel",
        out_shape=(f32(1, width, width), f32(1, width, width), f32(width, width)),
        in_specs=[VMEM] * (groups + 3),
        out_specs=(VMEM,) * 3,
        scratch_shapes=[pltpu.VMEM((width, 2 * width), jnp.float32)],
        cost_estimate=cost(2 * 3 * width**3 * 4, 4 * 8 * width * width),
    )(*ys, inverse_one, inverse_two, parent_two)
    diag_one, diag_two, par_two = pl.pallas_call(
        functools.partial(diag_kernel, groups),
        name="diag",
        out_shape=(f32(1, width, width),) * 3,
        in_specs=[VMEM] * (groups + 3),
        out_specs=(VMEM,) * 3,
        scratch_shapes=[pltpu.VMEM((width, width), jnp.float32)] * 2,
        cost_estimate=cost(2 * 3 * width**3 * 9, 4 * 9 * width * width),
    )(*totals, inverse_one, inverse_two, u_par)
    return diag_one, off_one, diag_two, par_two, root_two


def solution(mesh):
    return jax.shard_map(
        per_device,
        mesh=mesh,
        in_specs=(
            P("sn", None),
            P(),
            P("sn", "blk", None),
            P("sn", None, None),
            P("sn", None, None),
            P("sn", "blk", None),
            P("sn", None, None),
        ),
        out_specs=(
            P("sn", None, None),
            P("sn", "blk", None),
            P("sn", None, None),
            P("sn", None, None),
            P("sn", "blk", None),
        ),
        check_vma=False,
    )
```
